512 devices in a mesh: dp: 128 (over x, z, core), mp: 4 (over y).
Axes of the slice: x: 4, y: 4, z: 16, core: 2. Of those that a mesh axis runs over, the one named last changes fastest.
Arguments:
- frames: bfloat16 [32768, 2, 16, 256], P('dp', None, None, 'mp')
- cache: bfloat16 [32768, 2, 16, 256], P('dp', None, None, 'mp'), may hold values from -6 to 6
- group_offset: int32 [128], replicated, may hold values from 0 to 127, as said below
- cache_offset: int32 [128], replicated, may hold values from 0 to 127, as said below
- cache_group: int32 [128], replicated, may hold values from 0 to 127, each once
- group_rows: int32 [128, 128], P('dp'), may hold values from 1 to 2, 192 in all within a row
- cache_live: int32 [16384], P('dp'), may hold values 0 or 1
- temporal_weight: bfloat16 [3, 256, 512], P(None, None, 'mp')
- spatial_weight: bfloat16 [3, 512, 512], P(None, None, 'mp'), may hold values from -0.15625 to 0.15625
- norm_gain: bfloat16 [512], P('mp'), may hold values from 0.25 to 1.75
Outputs:
- latents: bfloat16 [32768, 2, 16, 512], P('dp', None, None, 'mp')
The draws below stay inside these ranges and needn't reach their ends.
Inputs may be any that keep to these rules, and one draw needn't show every extreme that they name: group_offset[g] equals group_offset[g2] exactly when g - g2 is a multiple of 128. cache_offset[h] equals cache_offset[h2] exactly when h - h2 is a multiple of 128.
All inputs are finite; a program needn't handle non-finite values. No bound on the sum of `cache_live` on one device may be relied on, other than what follows from the above.
Results may differ from the reference program's by a relative error of at most 0.0026.
Values may be sent and summed in bfloat16 or wider, within the bound.
A program may use at most 128 MiB of HBM per device.

```python
import math
import jax
import jax.numpy as jnp
import numpy as np
from jax import lax

C_IN = 256
C = 512
W = 16
TS = 2
K = 3
P_SIZE = 2
G = 128
N_DP = 128


def draw_frames(key, part):
    first, second = jax.random.split(key, 2)
    shape = (N_DP * G * P_SIZE, TS, W, C_IN)
    base = jnp.clip(jax.random.normal(first, shape, jnp.float32), -6.0, 6.0)
    scale = 10.0 ** jax.random.uniform(second, (N_DP * G * P_SIZE, TS, W, 1), jnp.float32, -0.5, 0.5)
    return (base * scale).astype(jnp.bfloat16)


def draw_temporal_weight(key, part):
    first, second = jax.random.split(key)
    base = jnp.clip(jax.random.normal(first, (K, C_IN, C), jnp.float32), -6.0, 6.0) * (K * C_IN) ** (-0.5)
    column = jnp.arange(C, dtype=jnp.float32) / C - 0.5
    rough = jnp.exp(jax.random.uniform(second, (1, 1, C), jnp.float32, -0.4, 0.4))
    return (base * (10.0 ** column)[None, None, :] * rough).astype(jnp.bfloat16)


def offset_table(key):
    first, second = jax.random.split(key)
    values = jnp.arange(N_DP, dtype=jnp.int32)
    scores = jax.random.permutation(first, N_DP).astype(jnp.int32)
    forced = (values == 1) | (values == N_DP // 2)
    scores = jnp.where(forced, scores - 2 * N_DP, scores)
    ordered = values[jnp.argsort(scores, stable=True)]
    used = min(G, N_DP)
    leading = ordered[:used]
    placed = leading[jax.random.permutation(second, used).astype(jnp.int32)]
    return placed[jnp.arange(G, dtype=jnp.int32) % used].astype(jnp.int32)


def draw_group_offset(key, part):
    return offset_table(jax.random.fold_in(key, 11))


def draw_cache_offset(key, part):
    return offset_table(jax.random.fold_in(key, 23))


def place_ends(drawn, stream_key, low, top_value):
    longest = drawn.shape.index(max(drawn.shape))
    spots = []
    for shift in (0, 1):
        where = [jax.random.randint(jax.random.fold_in(stream_key, axis), (), 0, length) for axis, length in enumerate(drawn.shape)]
        where[longest] = (where[longest] + shift) % drawn.shape[longest]
        spots.append(tuple(where))
    return drawn.at[spots[0]].set(low).at[spots[1]].set(top_value)


def levels(own_key, extent, cuts, least, largest):
    gain, own = 1.0, jax.random.fold_in(own_key, 6)
    for position, shards_of in cuts:
        steps = jnp.exp(jax.random.uniform(jax.random.fold_in(own, position), (shards_of,), jnp.float32, least / len(cuts), largest / len(cuts)))
        gain = gain * jnp.repeat(steps, extent[position] // shards_of).reshape([-1 if axis == position else 1 for axis in range(len(extent))])
    return gain


def length_profile(count, total, most, lean):
    loads = [(1 << 20) // math.isqrt(rank ** lean) + 1 for rank in range(2, count + 1)]
    spare, holding = total - most - (count - 1), [1] * (count - 1)
    while spare > 0:
        free = [i for i in range(count - 1) if holding[i] < most]
        pool, remaining = sum([loads[i] for i in free]), spare
        for i in free:
            extra = min(most - holding[i], max(1, remaining * loads[i] // pool), spare)
            holding[i] = holding[i] + extra
            spare = spare - extra
    return np.array([most] + holding)


def uneven_parts(rng, number_of, total, bound, slope):
    if number_of == 2:
        one = jax.random.randint(rng, (), max(1, total - bound), min(bound, total - 1) + 1)
        return jnp.stack([one, total - one])
    tallies = jnp.asarray(length_profile(number_of, total, bound, slope), jnp.int32)
    couples = (number_of - 1) // 2
    source_of, taker = tallies[1:1 + 2 * couples:2], tallies[2:2 + 2 * couples:2]
    margin = jnp.minimum(source_of - 1, bound - taker)
    passed = jax.random.randint(jax.random.fold_in(rng, 1), (couples,), 0, 1 << 20) % (margin + 1)
    tallies = tallies.at[1:1 + 2 * couples:2].set(source_of - passed).at[2:2 + 2 * couples:2].set(taker + passed)
    return tallies[jax.random.permutation(jax.random.fold_in(rng, 2), number_of)]


def scatter_about(own_key, extent, spread, limit, cuts=(), kind=jnp.bfloat16):
    array = spread * jax.random.normal(own_key, extent, jnp.float32)
    if cuts:
        array = array * levels(own_key, extent, cuts, -0.22, 0.18)
    return jnp.clip(array, -limit, limit).astype(kind)


def setup_inputs(seed: int = 0) -> dict:
    seeds = jax.random.split(jax.random.key(seed), 11)
    frames = draw_frames(jax.random.fold_in(seeds[10], 71), 0)
    cache = scatter_about(seeds[1], (N_DP * G * P_SIZE, K - 1, W, C_IN), 1.0, 6.0, ((0, 128), (3, 4)))
    group_offset = draw_group_offset(jax.random.fold_in(seeds[10], 71), 0)
    cache_offset = draw_cache_offset(jax.random.fold_in(seeds[10], 71), 0)
    cache_group = jax.random.permutation(seeds[4], G).astype(jnp.int32)
    group_rows = jax.vmap(lambda own: uneven_parts(own, G, (P_SIZE + 1) * G // 2, P_SIZE, 1))(jax.random.split(seeds[5], N_DP)).reshape((N_DP, G)).astype(jnp.int32)
    cache_live = place_ends((jax.random.randint(seeds[6], (N_DP * G,), 0, 4) < 3).astype(jnp.int32), jax.random.fold_in(seeds[6], 1), 0, 1)
    temporal_weight = draw_temporal_weight(jax.random.fold_in(seeds[10], 71), 0)
    spatial_weight = scatter_about(seeds[8], (3, C, C), (3 * C) ** -0.5, 0.15625, ((2, 4),))
    norm_gain = jnp.clip(1.0 + 0.15 * jax.random.normal(seeds[9], (C,), jnp.float32), 0.25, 1.75).astype(jnp.bfloat16)
    return dict(frames=frames, cache=cache, group_offset=group_offset, cache_offset=cache_offset, cache_group=cache_group, group_rows=group_rows, cache_live=cache_live, temporal_weight=temporal_weight, spatial_weight=spatial_weight, norm_gain=norm_gain)


def reference(frames, cache, group_offset, cache_offset, cache_group, group_rows, cache_live, temporal_weight, spatial_weight, norm_gain):
    stored = frames.reshape(N_DP, G, P_SIZE, TS, W, C_IN)
    carried_all = cache.reshape(N_DP, G, P_SIZE, K - 1, W, C_IN)
    live_all = cache_live.reshape(N_DP, G)
    owner_ids = jnp.arange(N_DP, dtype=jnp.int32)
    group_ids = jnp.arange(G, dtype=jnp.int32)
    inverse = lax.optimization_barrier(jnp.sum(group_ids[:, None] * (cache_group[:, None] == group_ids[None, :]).astype(jnp.int32), axis=0)).astype(jnp.int32)
    sources = (owner_ids[:, None] - group_offset[None, :]) % N_DP
    previous = (owner_ids[:, None] - cache_offset[inverse][None, :]) % N_DP
    time_weight = temporal_weight.astype(jnp.float32)
    space_weight = spatial_weight.astype(jnp.float32)
    gain_full = norm_gain.astype(jnp.float32)

    def encode(owner):
        source_row = sources[owner]
        prev_row = previous[owner]
        rows = stored[source_row, group_ids]
        counts = group_rows[source_row, group_ids]
        carried = carried_all[prev_row, inverse]
        flags = live_all[prev_row, inverse]
        carried = jnp.where(flags[:, None, None, None, None] > 0, carried, jnp.zeros_like(carried))
        sequence = jnp.concatenate([carried, rows], axis=2).astype(jnp.float32)
        conv_time = jnp.zeros((G, P_SIZE, TS, W, C), jnp.float32)
        for tap_index in range(K):
            window = sequence[:, :, K - 1 - tap_index:K - 1 - tap_index + TS]
            conv_time = conv_time + jnp.einsum('gptwc,cd->gptwd', window, time_weight[tap_index])
        mean_square = lax.optimization_barrier(jnp.mean(conv_time * conv_time, axis=-1, keepdims=True))
        activated = jax.nn.silu(conv_time * lax.rsqrt(mean_square + 1e-06) * gain_full).astype(jnp.bfloat16)
        padded = jnp.pad(activated, ((0, 0), (0, 0), (0, 0), (1, 1), (0, 0))).astype(jnp.float32)
        conv_space = jnp.zeros((G, P_SIZE, TS, W, C), jnp.float32)
        for tap_index in range(3):
            conv_space = conv_space + jnp.einsum('gptwc,cd->gptwd', padded[:, :, :, tap_index:tap_index + W], space_weight[tap_index])
        live_rows = jnp.arange(P_SIZE, dtype=jnp.int32)[None, :] < counts[:, None]
        total = jnp.where(live_rows[:, :, None, None, None], conv_time + conv_space, 0.0)
        return total.astype(jnp.bfloat16)
    encoded = lax.map(encode, owner_ids)
    return encoded.reshape(N_DP * G * P_SIZE, TS, W, C)
```

```python
import functools

import jax
import jax.numpy as jnp
from jax import lax
from jax.experimental import pallas as pl
from jax.experimental.pallas import tpu as pltpu
from jax.sharding import PartitionSpec as P

MESH = pl.DeviceIdType.MESH
EPS = 1e-6


def grid_of(owners):
    x_size = max(1, owners // 32)
    return x_size, owners // (2 * x_size)


def pair_number(source, owner, owners):
    x_size, z_size = grid_of(owners)
    half = z_size // 2
    dc = (owner % 2 - source % 2) % 2
    dz = (owner // 2 % z_size - source // 2 % z_size) % z_size
    dx = (owner // (2 * z_size) - source // (2 * z_size)) % x_size
    b = (dz >= half).astype(jnp.int32)
    h = jnp.where(dz >= half, z_size - 1 - dz, dz)
    c = (dx - h) % x_size
    return ((c * half + h) * 2 + dc) * 2 + b


def compute_slot(n, owners, ranks):
    half = grid_of(owners)[1] // 2
    b, dc, h, c = n % 2, n // 2 % 2, n // 4 % half, n // (4 * half)
    rank = (c + 2 * dc + h % 2) % ranks
    return rank * (owners // ranks) + c * half + h // 2 * 2 + b


def exchange_kernel(
    sizes, slot_of, keys, xc, xf, wt, ws, gn, out,
    wide, cache_out, frames_out, cache_in, cache_turn, carried, rows, wt_all, ws_all, gn_all, taps, result,
    w_send, w_recv, c_send, c_recv, f_send, f_recv, y_send, y_recv, o_send, o_recv,
):
    owners, ranks, pair, steps, width, cut, channels = sizes
    x_size, z_size = grid_of(owners)
    half = z_size // 2
    slots = owners // ranks
    part = channels // ranks
    c_in = cut * ranks
    lanes = steps * cut
    block = pair * width
    me, mine = lax.axis_index("dp"), lax.axis_index("mp")
    my_c, my_z, my_x = lax.rem(me, 2), lax.rem(lax.div(me, 2), z_size), lax.div(me, 2 * z_size)
    my_columns = pl.ds(pl.multiple_of(mine * part, part), part)

    def split(n):
        return lax.rem(n, 2), lax.rem(lax.div(n, 2), 2), lax.rem(lax.div(n, 4), half), lax.div(n, 4 * half)

    def owner_of(n):
        b, dc, h, c = split(n)
        z = lax.rem(my_z + h + b * (z_size - 1 - 2 * h), z_size)
        x = lax.rem(my_x + lax.rem(c + h, x_size), x_size)
        return (x * z_size + z) * 2 + lax.rem(my_c + dc, 2)

    weights = ((wt, wt_all), (ws, ws_all), (gn, gn_all))
    for index, (own, whole) in enumerate(weights):
        for turn in range(1, ranks):
            pltpu.make_async_remote_copy(
                own, whole.at[:, my_columns], w_send.at[index], w_recv.at[index],
                device_id=(me, lax.rem(mine + turn, ranks)), device_id_type=MESH,
            ).start()
        pltpu.make_async_copy(own, whole.at[:, my_columns], w_recv.at[index]).start()

    def pack(x, place, goes):
        for w in range(width):
            columns = jnp.concatenate(
                [x[(t * width + w) * cut : (t * width + w + 1) * cut, :] for t in range(steps)], axis=0
            )
            wide[pl.ds(w, owners * pair, stride=width), :] = lax.dot_general(
                place, columns, (((1,), (1,)), ((), ())), preferred_element_type=jnp.float32
            )

        per = min(16, owners)

        def narrow(i, _):
            piece = wide[pl.ds(pl.multiple_of(i * (per * block), per * block), per * block), :]
            goes[pl.ds(i * per, per)] = piece.astype(jnp.bfloat16).reshape(per, block, lanes)
            return 0

        lax.fori_loop(0, owners // per, narrow, 0)

    target = lax.broadcasted_iota(jnp.int32, (owners * pair, owners * pair), 0)
    pack(xc, jnp.where(target == keys[0:1, :], 1.0, 0.0).astype(jnp.bfloat16), cache_out)

    def send_cache(n, _):
        pltpu.make_async_remote_copy(
            cache_out.at[n], cache_in.at[n], c_send, c_recv, device_id=(owner_of(n), mine), device_id_type=MESH
        ).start()
        return 0

    lax.fori_loop(1, owners, send_cache, 0)

    live = jnp.where(keys[2:3, :] > 0, 1.0, jnp.nan)
    pack(xf, jnp.where(target == keys[1:2, :], live, 0.0).astype(jnp.bfloat16), frames_out)

    def frames_copy(n):
        b, dc, h, c = split(n)
        rank = lax.rem(c + 2 * dc + lax.rem(h, 2), ranks)
        place = c * half + lax.div(h, 2) * 2 + b
        return pltpu.make_async_remote_copy(
            frames_out.at[n], rows.at[mine, place], f_send, f_recv.at[c],
            device_id=(owner_of(n), rank), device_id_type=MESH,
        )

    @pl.when(mine == 0)
    def _():
        pltpu.make_async_copy(frames_out.at[0], rows.at[0, 0], f_recv.at[0]).start()

    @pl.when(mine != 0)
    def _():
        frames_copy(0).start()

    def send_frames(n, _):
        frames_copy(n).start()
        return 0

    lax.fori_loop(1, owners, send_frames, 0)

    for index, (own, whole) in enumerate(weights):
        pltpu.make_async_copy(whole, whole, w_recv.at[index]).wait()
    for m in range(ranks):
        tap = [wt_all[k * c_in + m * cut : k * c_in + (m + 1) * cut, :] for k in range(3)]
        nothing = jnp.zeros_like(tap[0])
        table = ((tap[0], tap[1]), (nothing, tap[0]), (tap[2], nothing), (tap[1], tap[2]))
        for q, (first, second) in enumerate(table):
            start = (q // 2 * ranks + m) * lanes + q % 2 * cut
            taps[start : start + cut, :channels] = first
            taps[start : start + cut, channels:] = second

    others = pl.ds(1, owners - 1)
    pltpu.make_async_copy(cache_in.at[others], cache_in.at[others], c_recv).wait()
    cache_in[0] = cache_out[0]

    def turn_cache(i, _):
        cache_turn[lax.div(i, slots), lax.rem(i, slots)] = cache_in[slot_of[i]]
        return 0

    lax.fori_loop(0, owners, turn_cache, 0)
    for turn in range(1, ranks):
        peer = lax.rem(mine + turn, ranks)
        pltpu.make_async_remote_copy(
            cache_turn.at[peer], carried.at[mine], y_send, y_recv, device_id=(me, peer), device_id_type=MESH
        ).start()
    pltpu.make_async_copy(cache_turn.at[mine], carried.at[mine], y_recv).start()
    pltpu.make_async_copy(carried, carried, y_recv).wait()

    gain = gn_all[0:1, :].astype(jnp.float32)
    tokens = half * block
    spot = lax.rem(lax.broadcasted_iota(jnp.int32, (steps * tokens, 1), 0), width)

    def encode(c, _):
        here = pl.ds(c * half, half)
        pltpu.make_async_copy(rows.at[:, here], rows.at[:, here], f_recv.at[c]).wait()
        pieces = [rows[m, here].reshape(tokens, lanes) for m in range(ranks)]
        dead = pieces[0][:, 0:1].astype(jnp.float32)
        dead = dead != dead
        pieces = pieces + [carried[m, here].reshape(tokens, lanes) for m in range(ranks)]
        both = jnp.dot(jnp.concatenate(pieces, axis=1), taps[...], preferred_element_type=jnp.float32)
        conv = jnp.concatenate([both[:, :channels], both[:, channels:]], axis=0)
        scale = lax.rsqrt(jnp.sum(conv * conv, axis=1, keepdims=True) / channels + EPS)
        scaled = conv * scale * gain
        active = scaled * (1.0 / (1.0 + jnp.exp(-scaled)))
        before = jnp.where(spot == 0, 0.0, pltpu.roll(active, 1, 0))
        after = jnp.where(spot == width - 1, 0.0, pltpu.roll(active, steps * tokens - 1, 0))
        joined = jnp.concatenate([v.astype(jnp.bfloat16) for v in (before, active, after)], axis=1)
        total = conv + jnp.dot(joined, ws_all[...], preferred_element_type=jnp.float32)
        total = jnp.where(jnp.concatenate([dead] * steps, axis=0), 0.0, total).astype(jnp.bfloat16)
        for m in range(ranks):
            for t in range(steps):
                piece = total[t * tokens : (t + 1) * tokens, m * part : (m + 1) * part]
                result[m, here, :, t] = piece.reshape(half, pair, width, part)
        for turn in range(1, ranks):
            peer = lax.rem(mine + turn, ranks)
            pltpu.make_async_remote_copy(
                result.at[peer, here], out.at[mine, here], o_send, o_recv, device_id=(me, peer), device_id_type=MESH
            ).start()
        pltpu.make_async_copy(result.at[mine, here], out.at[mine, here], o_recv).start()
        return 0

    lax.fori_loop(0, x_size, encode, 0)

    for index, (own, whole) in enumerate(weights):
        sent = whole.at[:, pl.ds(0, (ranks - 1) * part)]
        pltpu.make_async_copy(sent, sent, w_send.at[index]).wait()
    pltpu.make_async_copy(cache_out.at[others], cache_out.at[others], c_send).wait()

    @pl.when(mine == 0)
    def _():
        pltpu.make_async_copy(frames_out.at[others], frames_out.at[others], f_send).wait()

    @pl.when(mine != 0)
    def _():
        pltpu.make_async_copy(frames_out, frames_out, f_send).wait()

    sent = cache_turn.at[pl.ds(0, ranks - 1)]
    pltpu.make_async_copy(sent, sent, y_send).wait()
    sent = result.at[pl.ds(0, ranks - 1)]
    pltpu.make_async_copy(sent, sent, o_send).wait()
    pltpu.make_async_copy(out, out, o_recv).wait()


def order_kernel(per, slot_of, got, out):
    first = pl.program_id(0) * per

    def place(i, _):
        out[i] = got[slot_of[first + i]]
        return 0

    lax.fori_loop(0, per, place, 0)


def local(
    owners, ranks,
    frames, cache, group_offset, cache_offset, cache_group, group_rows, cache_live,
    temporal_weight, spatial_weight, norm_gain,
):
    me = lax.axis_index("dp")
    groups = group_offset.shape[0]
    pair = frames.shape[0] // groups
    steps, width, cut = frames.shape[1:]
    channels, part = spatial_weight.shape[1:]
    slots = owners // ranks
    group_index = jnp.arange(groups, dtype=jnp.int32)
    second = jnp.arange(pair, dtype=jnp.int32)[None, :]

    frames_to = pair_number(me, (me + group_offset) % owners, owners)
    cache_to = pair_number(me, (me + cache_offset) % owners, owners)
    keys = jnp.stack(
        [
            jnp.where(cache_live[:, None] > 0, cache_to[:, None] * pair + second, -1).reshape(-1),
            (frames_to[:, None] * pair + second).reshape(-1),
            (second < group_rows.reshape(groups)[:, None]).astype(jnp.int32).reshape(-1),
        ]
        + [jnp.zeros((groups * pair,), jnp.int32)] * 5
    )
    offset_here = jnp.sum(
        jnp.where(cache_group[:, None] == group_index[None, :], cache_offset[:, None], 0), axis=0
    )
    own_slot = compute_slot(pair_number((me - group_offset) % owners, me, owners), owners, ranks)
    from_cache = pair_number((me - offset_here) % owners, me, owners)
    cache_slot = jnp.sum(jnp.where(own_slot[:, None] == group_index[None, :], from_cache[:, None], 0), axis=0)

    rows_minor = lambda x: jnp.transpose(x, (1, 2, 3, 0)).reshape(steps * width * cut, groups * pair)
    block, lanes = pair * width, steps * cut
    vmem, smem, anywhere = (pl.BlockSpec(memory_space=s) for s in (pltpu.VMEM, pltpu.SMEM, pl.ANY))
    bf16 = jnp.bfloat16
    dma = pltpu.SemaphoreType.DMA
    got = pl.pallas_call(
        functools.partial(exchange_kernel, (owners, ranks, pair, steps, width, cut, channels)),
        out_shape=jax.ShapeDtypeStruct((ranks, slots, pair, steps, width, part), bf16),
        in_specs=[smem, vmem, vmem, vmem, anywhere, anywhere, anywhere],
        out_specs=anywhere,
        scratch_shapes=[
            pltpu.VMEM((owners * block, lanes), jnp.float32),
            pltpu.VMEM((owners, block, lanes), bf16),
            pltpu.VMEM((owners, block, lanes), bf16),
            pltpu.VMEM((owners, block, lanes), bf16),
            pltpu.VMEM((ranks, slots, block, lanes), bf16),
            pltpu.VMEM((ranks, slots, block, lanes), bf16),
            pltpu.VMEM((ranks, slots, block, lanes), bf16),
            pltpu.VMEM((3 * cut * ranks, channels), bf16),
            pltpu.VMEM((3 * channels, channels), bf16),
            pltpu.VMEM((16, channels), bf16),
            pltpu.VMEM((2 * ranks * lanes, steps * channels), bf16),
            pltpu.VMEM((ranks, slots, pair, steps, width, part), bf16),
            dma((3,)), dma((3,)), dma(()), dma(()), dma(()), dma((grid_of(owners)[0],)),
            dma(()), dma(()), dma(()), dma(()),
        ],
        compiler_params=pltpu.CompilerParams(has_side_effects=True, vmem_limit_bytes=48 << 20),
        name="exchange",
    )(
        cache_slot, keys, rows_minor(cache), rows_minor(frames),
        temporal_weight.reshape(-1, part), spatial_weight.reshape(-1, part),
        jnp.broadcast_to(norm_gain[None, :], (16, part)),
    )
    tokens = pair * steps * width
    per = min(32, groups)
    ordered = pl.pallas_call(
        functools.partial(order_kernel, per),
        out_shape=jax.ShapeDtypeStruct((groups, tokens, part), bf16),
        grid_spec=pltpu.PrefetchScalarGridSpec(
            num_scalar_prefetch=1,
            grid=(groups // per,),
            in_specs=[pl.BlockSpec((groups, tokens, part), lambda i, s: (0, 0, 0))],
            out_specs=pl.BlockSpec((per, tokens, part), lambda i, s: (i, 0, 0)),
        ),
        name="order",
    )(own_slot, got.reshape(groups, tokens, part))
    return ordered.reshape(groups * pair, steps, width, part)


def solution(mesh):
    in_specs = (
        P("dp", None, None, "mp"),
        P("dp", None, None, "mp"),
        P(),
        P(),
        P(),
        P("dp", None),
        P("dp"),
        P(None, None, "mp"),
        P(None, None, "mp"),
        P("mp"),
    )
    out_specs = P("dp", None, None, "mp")
    body = functools.partial(local, mesh.shape["dp"], mesh.shape["mp"])
    return jax.shard_map(body, mesh=mesh, in_specs=in_specs, out_specs=out_specs, check_vma=False)
```

```python
import functools

import jax
import jax.numpy as jnp
from jax import lax
from jax.experimental import pallas as pl
from jax.experimental.pallas import tpu as pltpu
from jax.sharding import PartitionSpec as P

MESH = pl.DeviceIdType.MESH
EPS = 1e-6


def grid_of(owners):
    x_size = max(1, owners // 32)
    return x_size, owners // (2 * x_size)


def log2(size):
    return size.bit_length() - 1


def pair_number(source, owner, owners):
    x_size, z_size = grid_of(owners)
    half = z_size // 2
    dc = (owner - source) & 1
    dz = ((owner >> 1) - (source >> 1)) & (z_size - 1)
    dx = ((owner >> log2(2 * z_size)) - (source >> log2(2 * z_size))) & (x_size - 1)
    b = jnp.where(dz >= half, 1, 0)
    h = jnp.where(dz >= half, z_size - 1 - dz, dz)
    c = (dx - h) & (x_size - 1)
    return ((c * half + h) * 2 + dc) * 2 + b


def compute_slot(n, owners, ranks):
    half = grid_of(owners)[1] // 2
    b, dc, h, c = n & 1, (n >> 1) & 1, (n >> 2) & (half - 1), n >> log2(4 * half)
    rank = (c + 2 * dc + (h & 1)) & (ranks - 1)
    return rank * (owners // ranks) + c * half + (h >> 1) * 2 + b


def exchange_kernel(
    sizes, goes_to, cache_goes_to, continues, counts, lives, xc, xf, wt, ws, gn, out, order_out,
    table, picks, slot_row, slot_of, wide, xc_in, xf_in, gn_own, gn_row,
    cache_out, frames_out, cache_in, cache_turn, carried, rows, wt_all, ws_all, gn_all, taps, result,
    x_sem, t_sem, w_send, w_recv, c_send, c_recv, f_send, f_recv, y_send, y_recv, o_send, o_recv, ready,
):
    owners, ranks, pair, steps, width, cut, channels = sizes
    x_size, z_size = grid_of(owners)
    half = z_size // 2
    slots = owners // ranks
    stages = x_size * min(2, half // 2)
    part = channels // ranks
    c_in = cut * ranks
    lanes = steps * cut
    block = pair * width
    me, mine = lax.axis_index("dp"), lax.axis_index("mp")
    my_c, my_z, my_x = lax.rem(me, 2), lax.rem(lax.div(me, 2), z_size), lax.div(me, 2 * z_size)
    my_columns = pl.ds(pl.multiple_of(mine * part, part), part)
    bf16, f32 = jnp.bfloat16, jnp.float32

    loads = [
        pltpu.make_async_copy(own, here, x_sem.at[i])
        for i, (own, here) in enumerate(
            [(xc, xc_in), (xf, xf_in), (gn, gn_row)]
            + [(v, table.at[i]) for i, v in enumerate((goes_to, cache_goes_to, continues, counts, lives))]
        )
    ]
    for load in loads[3:] + loads[:3]:
        load.start()

    barrier = pltpu.get_barrier_semaphore()

    def greet(i, _):
        pl.semaphore_signal(barrier, inc=1, device_id=(lax.rem(me + i, owners), mine), device_id_type=MESH)
        return 0

    lax.fori_loop(1, owners, greet, 0)
    for turn in range(1, ranks):
        pl.semaphore_signal(
            barrier, inc=1, device_id=(me, lax.rem(mine + turn, ranks)), device_id_type=MESH
        )

    def split(n):
        return lax.rem(n, 2), lax.rem(lax.div(n, 2), 2), lax.rem(lax.div(n, 4), half), lax.div(n, 4 * half)

    def owner_of(n):
        b, dc, h, c = split(n)
        z = lax.rem(my_z + h + b * (z_size - 1 - 2 * h), z_size)
        x = lax.rem(my_x + lax.rem(c + h, x_size), x_size)
        return (x * z_size + z) * 2 + lax.rem(my_c + dc, 2)

    for load in loads[3:]:
        load.wait()
    group_to, cache_to, group_of, count, live = (table[i] for i in range(5))
    frames_n = pair_number(me, (me + group_to) & (owners - 1), owners)
    cache_n = pair_number(me, (me + cache_to) & (owners - 1), owners)
    sort = lax.broadcasted_iota(jnp.int32, (8, owners), 0)
    stack = jnp.where(sort == 0, frames_n, jnp.where(sort == 1, cache_n, jnp.where(sort == 2, count, live)))
    spread = lax.broadcasted_iota(jnp.int32, (owners, owners * pair), 1) >> log2(pair)
    spread = spread == lax.broadcasted_iota(jnp.int32, (owners, owners * pair), 0)
    one_hot = lambda mask: jnp.where(mask, 1.0, 0.0).astype(bf16)
    keys = jnp.dot(stack.astype(f32).astype(bf16), one_hot(spread), preferred_element_type=f32)
    second = (lax.broadcasted_iota(jnp.int32, (1, owners * pair), 1) & (pair - 1)).astype(f32)
    target = lax.broadcasted_iota(jnp.int32, (owners * pair, owners * pair), 0).astype(f32)

    def pack(x, place, goes):
        for w in range(width):
            columns = jnp.concatenate(
                [x[(t * width + w) * cut : (t * width + w + 1) * cut, :] for t in range(steps)], axis=0
            )
            wide[pl.ds(w, owners * pair, stride=width), :] = lax.dot_general(
                place, columns, (((1,), (1,)), ((), ())), preferred_element_type=f32
            )

        per = min(16, owners)

        def narrow(i, _):
            piece = wide[pl.ds(pl.multiple_of(i * (per * block), per * block), per * block), :]
            goes[pl.ds(i * per, per)] = piece.astype(bf16).reshape(per, block, lanes)
            return 0

        lax.fori_loop(0, owners // per, narrow, 0)

    loads[0].wait()
    pack(xc_in, jnp.where(target == keys[1:2, :] * pair + second, keys[3:4, :], 0.0).astype(bf16), cache_out)

    pl.semaphore_wait(barrier, owners - 1 + ranks - 1)
    for turn in range(1, ranks):
        pl.semaphore_signal(ready, inc=1, device_id=(me, lax.rem(mine + turn, ranks)), device_id_type=MESH)

    def send_cache(i, _):
        n = owners - 1 - i
        pltpu.make_async_remote_copy(
            cache_out.at[n], cache_in.at[n], c_send, c_recv, device_id=(owner_of(n), mine), device_id_type=MESH
        ).start()
        return 0

    lax.fori_loop(0, owners - 1, send_cache, 0)

    loads[1].wait()
    valid = jnp.where(second < keys[2:3, :], 1.0, jnp.nan)
    pack(xf_in, jnp.where(target == keys[0:1, :] * pair + second, valid, 0.0).astype(bf16), frames_out)

    def frames_copy(n):
        b, dc, h, c = split(n)
        rank = lax.rem(c + 2 * dc + lax.rem(h, 2), ranks)
        place = c * half + lax.div(h, 2) * 2 + b
        return pltpu.make_async_remote_copy(
            frames_out.at[n], rows.at[mine, place], f_send, f_recv.at[lax.div(n, owners // stages)],
            device_id=(owner_of(n), rank), device_id_type=MESH,
        )

    pl.semaphore_wait(ready, ranks - 1)

    def send_frames(i, _):
        frames_copy(owners - 1 - i).start()
        return 0

    lax.fori_loop(0, owners - 1, send_frames, 0)

    @pl.when(mine == 0)
    def _():
        pltpu.make_async_copy(frames_out.at[0], rows.at[0, 0], f_recv.at[0]).start()

    @pl.when(mine != 0)
    def _():
        frames_copy(0).start()

    loads[2].wait()
    gn_own[...] = jnp.broadcast_to(gn_row[...].astype(f32), gn_own.shape).astype(bf16)
    weights = ((wt, wt_all), (ws, ws_all), (gn_own, gn_all))
    for index, (own, whole) in enumerate(weights):
        for turn in range(1, ranks):
            pltpu.make_async_remote_copy(
                own, whole.at[:, my_columns], w_send.at[index], w_recv.at[index],
                device_id=(me, lax.rem(mine + turn, ranks)), device_id_type=MESH,
            ).start()
        pltpu.make_async_copy(own, whole.at[:, my_columns], w_recv.at[index]).start()

    own_n = pair_number((me - group_to) & (owners - 1), me, owners)
    own_slot = compute_slot(own_n, owners, ranks)
    slot_row[...] = own_slot
    slot_store = pltpu.make_async_copy(slot_row, order_out, t_sem.at[1])
    slot_store.start()
    line = lax.broadcasted_iota(jnp.int32, (owners, owners), 0)

    def choose(values, mask):
        values = jnp.broadcast_to(values.astype(f32), (8, owners)).astype(bf16)
        got = lax.dot_general(values, one_hot(mask), (((1,), (1,)), ((), ())), preferred_element_type=f32)
        return got[0:1, :].astype(jnp.int32)

    cache_here = choose(cache_to, line == group_of)
    cache_from = pair_number((me - cache_here) & (owners - 1), me, owners)
    picks[...] = choose(cache_from, line == own_slot)
    pick_load = pltpu.make_async_copy(picks, slot_of, t_sem.at[0])
    pick_load.start()

    for index, (own, whole) in enumerate(weights):
        pltpu.make_async_copy(whole, whole, w_recv.at[index]).wait()
    for m in range(ranks):
        tap = [wt_all[k * c_in + m * cut : k * c_in + (m + 1) * cut, :] for k in range(3)]
        nothing = jnp.zeros_like(tap[0])
        table = ((tap[0], tap[1]), (nothing, tap[0]), (tap[2], nothing), (tap[1], tap[2]))
        for q, (first, second) in enumerate(table):
            start = (q // 2 * ranks + m) * lanes + q % 2 * cut
            taps[start : start + cut, :channels] = first
            taps[start : start + cut, channels:] = second

    others = pl.ds(1, owners - 1)
    pltpu.make_async_copy(cache_in.at[others], cache_in.at[others], c_recv).wait()
    cache_in[0] = cache_out[0]

    pick_load.wait()

    def turn_cache(i, _):
        cache_turn[lax.div(i, slots), lax.rem(i, slots)] = cache_in[jnp.minimum(jnp.maximum(slot_of[0, i], 0), owners - 1)]
        return 0

    lax.fori_loop(0, owners, turn_cache, 0)
    for turn in range(1, ranks):
        peer = lax.rem(mine + turn, ranks)
        pltpu.make_async_remote_copy(
            cache_turn.at[peer], carried.at[mine], y_send, y_recv, device_id=(me, peer), device_id_type=MESH
        ).start()
    pltpu.make_async_copy(cache_turn.at[mine], carried.at[mine], y_recv).start()
    pltpu.make_async_copy(carried, carried, y_recv).wait()

    gain = gn_all[0:1, :].astype(jnp.float32)
    size = slots // stages
    tokens = size * block
    spot = lax.rem(lax.broadcasted_iota(jnp.int32, (steps * tokens, 1), 0), width)

    def encode(i, _):
        stage = stages - 1 - i
        here = pl.ds(stage * size, size)
        pltpu.make_async_copy(rows.at[:, here], rows.at[:, here], f_recv.at[stage]).wait()
        pieces = [rows[m, here].reshape(tokens, lanes) for m in range(ranks)]
        dead = pieces[0][:, 0:1].astype(jnp.float32)
        dead = dead != dead
        pieces = pieces + [carried[m, here].reshape(tokens, lanes) for m in range(ranks)]
        both = jnp.dot(jnp.concatenate(pieces, axis=1), taps[...], preferred_element_type=jnp.float32)
        conv = jnp.concatenate([both[:, :channels], both[:, channels:]], axis=0)
        scale = lax.rsqrt(jnp.sum(conv * conv, axis=1, keepdims=True) / channels + EPS)
        scaled = conv * scale * gain
        active = scaled * (1.0 / (1.0 + jnp.exp(-scaled)))
        before = jnp.where(spot == 0, 0.0, pltpu.roll(active, 1, 0))
        after = jnp.where(spot == width - 1, 0.0, pltpu.roll(active, steps * tokens - 1, 0))
        joined = jnp.concatenate([v.astype(jnp.bfloat16) for v in (before, active, after)], axis=1)
        total = conv + jnp.dot(joined, ws_all[...], preferred_element_type=jnp.float32)
        total = jnp.where(jnp.concatenate([dead] * steps, axis=0), 0.0, total).astype(jnp.bfloat16)
        for m in range(ranks):
            for t in range(steps):
                piece = total[t * tokens : (t + 1) * tokens, m * part : (m + 1) * part]
                result[m, here, :, t] = piece.reshape(size, pair, width, part)
        for turn in range(1, ranks):
            peer = lax.rem(mine + turn, ranks)
            pltpu.make_async_remote_copy(
                result.at[peer, here], out.at[mine, here], o_send, o_recv, device_id=(me, peer), device_id_type=MESH
            ).start()
        pltpu.make_async_copy(result.at[mine, here], out.at[mine, here], o_recv).start()
        return 0

    lax.fori_loop(0, stages, encode, 0)

    for index, (own, whole) in enumerate(weights):
        sent = whole.at[:, pl.ds(0, (ranks - 1) * part)]
        pltpu.make_async_copy(sent, sent, w_send.at[index]).wait()
    pltpu.make_async_copy(cache_out.at[others], cache_out.at[others], c_send).wait()

    @pl.when(mine == 0)
    def _():
        pltpu.make_async_copy(frames_out.at[others], frames_out.at[others], f_send).wait()

    @pl.when(mine != 0)
    def _():
        pltpu.make_async_copy(frames_out, frames_out, f_send).wait()

    sent = cache_turn.at[pl.ds(0, ranks - 1)]
    pltpu.make_async_copy(sent, sent, y_send).wait()
    sent = result.at[pl.ds(0, ranks - 1)]
    pltpu.make_async_copy(sent, sent, o_send).wait()
    slot_store.wait()
    pltpu.make_async_copy(out, out, o_recv).wait()


def order_kernel(slot_of, got, out, sem):
    def place(i, _):
        pltpu.make_async_copy(got.at[slot_of[0, i]], out.at[i], sem).start()
        return 0

    lax.fori_loop(0, out.shape[0], place, 0)
    pltpu.make_async_copy(got, out, sem).wait()


def local(
    owners, ranks,
    frames, cache, group_offset, cache_offset, cache_group, group_rows, cache_live,
    temporal_weight, spatial_weight, norm_gain,
):
    groups = group_offset.shape[0]
    pair = frames.shape[0] // groups
    steps, width, cut = frames.shape[1:]
    channels, part = spatial_weight.shape[1:]
    slots = owners // ranks
    stages = grid_of(owners)[0] * min(2, grid_of(owners)[1] // 4)
    rows_minor = lambda x: jnp.transpose(x, (1, 2, 3, 0)).reshape(steps * width * cut, groups * pair)
    line = lambda x: x.reshape(1, groups)
    block, lanes, tokens = pair * width, steps * cut, pair * steps * width
    smem, hbm = (pl.BlockSpec(memory_space=s) for s in (pltpu.SMEM, pltpu.HBM))
    bf16 = jnp.bfloat16
    dma = pltpu.SemaphoreType.DMA
    got, own_slot = pl.pallas_call(
        functools.partial(exchange_kernel, (owners, ranks, pair, steps, width, cut, channels)),
        out_shape=(
            jax.ShapeDtypeStruct((ranks, slots, pair, steps, width, part), bf16),
            jax.ShapeDtypeStruct((1, groups), jnp.int32),
        ),
        in_specs=[hbm] * 10,
        out_specs=(hbm, hbm),
        scratch_shapes=[
            pltpu.VMEM((5, 1, groups), jnp.int32),
            pltpu.VMEM((1, groups), jnp.int32),
            pltpu.VMEM((1, groups), jnp.int32),
            pltpu.SMEM((1, groups), jnp.int32),
            pltpu.VMEM((owners * block, lanes), jnp.float32),
            pltpu.VMEM((steps * width * cut, groups * pair), bf16),
            pltpu.VMEM((steps * width * cut, groups * pair), bf16),
            pltpu.VMEM((16, part), bf16),
            pltpu.VMEM((1, part), bf16),
            pltpu.VMEM((owners, block, lanes), bf16),
            pltpu.VMEM((owners, block, lanes), bf16),
            pltpu.VMEM((owners, block, lanes), bf16),
            pltpu.VMEM((ranks, slots, block, lanes), bf16),
            pltpu.VMEM((ranks, slots, block, lanes), bf16),
            pltpu.VMEM((ranks, slots, block, lanes), bf16),
            pltpu.VMEM((3 * cut * ranks, channels), bf16),
            pltpu.VMEM((3 * channels, channels), bf16),
            pltpu.VMEM((16, channels), bf16),
            pltpu.VMEM((2 * ranks * lanes, steps * channels), bf16),
            pltpu.VMEM((ranks, slots, pair, steps, width, part), bf16),
            dma((8,)), dma((2,)), dma((3,)), dma((3,)), dma(()), dma(()), dma(()), dma((stages,)),
            dma(()), dma(()), dma(()), dma(()), pltpu.SemaphoreType.REGULAR,
        ],
        compiler_params=pltpu.CompilerParams(
            collective_id=0, has_side_effects=True, vmem_limit_bytes=60 << 20
        ),
        name="exchange",
    )(
        line(group_offset), line(cache_offset), line(cache_group), line(group_rows), line(cache_live),
        rows_minor(cache), rows_minor(frames),
        temporal_weight.reshape(-1, part), spatial_weight.reshape(-1, part), norm_gain.reshape(1, part),
    )
    ordered = pl.pallas_call(
        order_kernel,
        out_shape=jax.ShapeDtypeStruct((groups, tokens, part), bf16),
        in_specs=[smem, hbm],
        out_specs=hbm,
        scratch_shapes=[dma(())],
        compiler_params=pltpu.CompilerParams(vmem_limit_bytes=60 << 20),
        name="order",
    )(own_slot, got.reshape(groups, tokens, part))
    return ordered.reshape(groups * pair, steps, width, part)


def solution(mesh):
    in_specs = (
        P("dp", None, None, "mp"),
        P("dp", None, None, "mp"),
        P(),
        P(),
        P(),
        P("dp", None),
        P("dp"),
        P(None, None, "mp"),
        P(None, None, "mp"),
        P("mp"),
    )
    out_specs = P("dp", None, None, "mp")
    body = functools.partial(local, mesh.shape["dp"], mesh.shape["mp"])
    return jax.shard_map(body, mesh=mesh, in_specs=in_specs, out_specs=out_specs, check_vma=False)
```

```python
import functools

import jax
import jax.numpy as jnp
from jax import lax
from jax.experimental import pallas as pl
from jax.experimental.pallas import tpu as pltpu
from jax.sharding import PartitionSpec as P

MESH = pl.DeviceIdType.MESH
EPS = 1e-6


def grid_of(owners):
    x_size = max(1, owners // 32)
    return x_size, owners // (2 * x_size)


def log2(size):
    return size.bit_length() - 1


def pair_number(source, owner, owners):
    x_size, z_size = grid_of(owners)
    half = z_size // 2
    dc = (owner - source) & 1
    dz = ((owner >> 1) - (source >> 1)) & (z_size - 1)
    dx = ((owner >> log2(2 * z_size)) - (source >> log2(2 * z_size))) & (x_size - 1)
    b = jnp.where(dz >= half, 1, 0)
    h = jnp.where(dz >= half, z_size - 1 - dz, dz)
    c = (dx - h) & (x_size - 1)
    return ((c * half + h) * 2 + dc) * 2 + b


def compute_slot(n, owners, ranks):
    half = grid_of(owners)[1] // 2
    b, dc, h, c = n & 1, (n >> 1) & 1, (n >> 2) & (half - 1), n >> log2(4 * half)
    rank = (c + 2 * dc + (h & 1)) & (ranks - 1)
    return rank * (owners // ranks) + c * half + (h >> 1) * 2 + b


def exchange_kernel(
    sizes, goes_to, cache_goes_to, continues, counts, lives, xc, xf, wt, ws, gn, out, order_out,
    table, picks, slot_row, slot_of, wide, xc_in, xf_in, gn_own, gn_row,
    cache_out, frames_out, cache_in, cache_turn, carried, rows, wt_all, ws_all, gn_all, taps, result,
    x_sem, t_sem, w_send, w_recv, c_send, c_recv, f_send, f_recv, y_send, y_recv, o_send, o_recv, ready,
):
    owners, ranks, pair, steps, width, cut, channels = sizes
    x_size, z_size = grid_of(owners)
    half = z_size // 2
    slots = owners // ranks
    stages = x_size * min(2, half // 2)
    part = channels // ranks
    c_in = cut * ranks
    lanes = steps * cut
    block = pair * width
    me, mine = lax.axis_index("dp"), lax.axis_index("mp")
    my_c, my_z, my_x = lax.rem(me, 2), lax.rem(lax.div(me, 2), z_size), lax.div(me, 2 * z_size)
    my_columns = pl.ds(pl.multiple_of(mine * part, part), part)
    bf16, f32 = jnp.bfloat16, jnp.float32

    loads = [
        pltpu.make_async_copy(own, here, x_sem.at[i])
        for i, (own, here) in enumerate(
            [(xc, xc_in), (xf, xf_in), (gn, gn_row)]
            + [(v, table.at[i]) for i, v in enumerate((goes_to, cache_goes_to, continues, counts, lives))]
        )
    ]
    for load in loads[3:] + loads[:3]:
        load.start()

    barrier = pltpu.get_barrier_semaphore()

    def greet(i, _):
        pl.semaphore_signal(barrier, inc=1, device_id=(lax.rem(me + i, owners), mine), device_id_type=MESH)
        return 0

    lax.fori_loop(1, owners, greet, 0)
    for turn in range(1, ranks):
        pl.semaphore_signal(
            barrier, inc=1, device_id=(me, lax.rem(mine + turn, ranks)), device_id_type=MESH
        )

    def split(n):
        return lax.rem(n, 2), lax.rem(lax.div(n, 2), 2), lax.rem(lax.div(n, 4), half), lax.div(n, 4 * half)

    def owner_of(n):
        b, dc, h, c = split(n)
        z = lax.rem(my_z + h + b * (z_size - 1 - 2 * h), z_size)
        x = lax.rem(my_x + lax.rem(c + h, x_size), x_size)
        return (x * z_size + z) * 2 + lax.rem(my_c + dc, 2)

    for load in loads[3:]:
        load.wait()
    group_to, cache_to, group_of, count, live = (table[i] for i in range(5))
    frames_n = pair_number(me, (me + group_to) & (owners - 1), owners)
    cache_n = pair_number(me, (me + cache_to) & (owners - 1), owners)
    sort = lax.broadcasted_iota(jnp.int32, (8, owners), 0)
    stack = jnp.where(sort == 0, frames_n, jnp.where(sort == 1, cache_n, jnp.where(sort == 2, count, live)))
    spread = lax.broadcasted_iota(jnp.int32, (owners, owners * pair), 1) >> log2(pair)
    spread = spread == lax.broadcasted_iota(jnp.int32, (owners, owners * pair), 0)
    one_hot = lambda mask: jnp.where(mask, 1.0, 0.0).astype(bf16)
    keys = jnp.dot(stack.astype(f32).astype(bf16), one_hot(spread), preferred_element_type=f32)
    second = (lax.broadcasted_iota(jnp.int32, (1, owners * pair), 1) & (pair - 1)).astype(f32)
    target = lax.broadcasted_iota(jnp.int32, (owners * pair, owners * pair), 0).astype(f32)

    def pack(x, place, goes):
        for w in range(width):
            columns = jnp.concatenate(
                [x[(t * width + w) * cut : (t * width + w + 1) * cut, :] for t in range(steps)], axis=0
            )
            wide[pl.ds(w, owners * pair, stride=width), :] = lax.dot_general(
                place, columns, (((1,), (1,)), ((), ())), preferred_element_type=f32
            )

        per = min(16, owners)

        def narrow(i, _):
            piece = wide[pl.ds(pl.multiple_of(i * (per * block), per * block), per * block), :]
            goes[pl.ds(i * per, per)] = piece.astype(bf16).reshape(per, block, lanes)
            return 0

        lax.fori_loop(0, owners // per, narrow, 0)

    loads[0].wait()
    pack(xc_in, jnp.where(target == keys[1:2, :] * pair + second, keys[3:4, :], 0.0).astype(bf16), cache_out)

    pl.semaphore_wait(barrier, owners - 1 + ranks - 1)
    for turn in range(1, ranks):
        pl.semaphore_signal(ready, inc=1, device_id=(me, lax.rem(mine + turn, ranks)), device_id_type=MESH)

    def send_cache(i, _):
        n = owners - 1 - i
        pltpu.make_async_remote_copy(
            cache_out.at[n], cache_in.at[n], c_send, c_recv, device_id=(owner_of(n), mine), device_id_type=MESH
        ).start()
        return 0

    lax.fori_loop(0, owners - 1, send_cache, 0)

    loads[1].wait()
    valid = jnp.where(second < keys[2:3, :], 1.0, jnp.nan)
    pack(xf_in, jnp.where(target == keys[0:1, :] * pair + second, valid, 0.0).astype(bf16), frames_out)

    def frames_copy(n):
        b, dc, h, c = split(n)
        rank = lax.rem(c + 2 * dc + lax.rem(h, 2), ranks)
        place = c * half + lax.div(h, 2) * 2 + b
        return pltpu.make_async_remote_copy(
            frames_out.at[n], rows.at[mine, place], f_send, f_recv.at[lax.div(n, owners // stages)],
            device_id=(owner_of(n), rank), device_id_type=MESH,
        )

    pl.semaphore_wait(ready, ranks - 1)

    def send_frames(i, _):
        frames_copy(owners - 1 - i).start()
        return 0

    lax.fori_loop(0, owners - 1, send_frames, 0)

    @pl.when(mine == 0)
    def _():
        pltpu.make_async_copy(frames_out.at[0], rows.at[0, 0], f_recv.at[0]).start()

    @pl.when(mine != 0)
    def _():
        frames_copy(0).start()

    loads[2].wait()
    gn_own[...] = jnp.broadcast_to(gn_row[...].astype(f32), gn_own.shape).astype(bf16)
    weights = ((wt, wt_all), (ws, ws_all), (gn_own, gn_all))
    for index, (own, whole) in enumerate(weights):
        for turn in range(1, ranks):
            pltpu.make_async_remote_copy(
                own, whole.at[:, my_columns], w_send.at[index], w_recv.at[index],
                device_id=(me, lax.rem(mine + turn, ranks)), device_id_type=MESH,
            ).start()
        pltpu.make_async_copy(own, whole.at[:, my_columns], w_recv.at[index]).start()

    own_n = pair_number((me - group_to) & (owners - 1), me, owners)
    own_slot = compute_slot(own_n, owners, ranks)
    slot_row[...] = own_slot
    slot_store = pltpu.make_async_copy(slot_row, order_out, t_sem.at[1])
    slot_store.start()
    line = lax.broadcasted_iota(jnp.int32, (owners, owners), 0)

    def choose(values, mask):
        values = jnp.broadcast_to(values.astype(f32), (8, owners)).astype(bf16)
        got = lax.dot_general(values, one_hot(mask), (((1,), (1,)), ((), ())), preferred_element_type=f32)
        return got[0:1, :].astype(jnp.int32)

    cache_here = choose(cache_to, line == group_of)
    cache_from = pair_number((me - cache_here) & (owners - 1), me, owners)
    picks[...] = choose(cache_from, line == own_slot)
    pick_load = pltpu.make_async_copy(picks, slot_of, t_sem.at[0])
    pick_load.start()

    for index, (own, whole) in enumerate(weights):
        pltpu.make_async_copy(whole, whole, w_recv.at[index]).wait()
    for m in range(ranks):
        tap = [wt_all[k * c_in + m * cut : k * c_in + (m + 1) * cut, :] for k in range(3)]
        nothing = jnp.zeros_like(tap[0])
        table = ((tap[0], tap[1]), (nothing, tap[0]), (tap[2], nothing), (tap[1], tap[2]))
        for q, (first, second) in enumerate(table):
            start = (q // 2 * ranks + m) * lanes + q % 2 * cut
            taps[start : start + cut, :channels] = first
            taps[start : start + cut, channels:] = second

    others = pl.ds(1, owners - 1)
    pltpu.make_async_copy(cache_in.at[others], cache_in.at[others], c_recv).wait()
    cache_in[0] = cache_out[0]

    pick_load.wait()

    def turn_cache(i, _):
        cache_turn[lax.div(i, slots), lax.rem(i, slots)] = cache_in[jnp.minimum(jnp.maximum(slot_of[0, i], 0), owners - 1)]
        return 0

    lax.fori_loop(0, owners, turn_cache, 0)
    for turn in range(1, ranks):
        peer = lax.rem(mine + turn, ranks)
        pltpu.make_async_remote_copy(
            cache_turn.at[peer], carried.at[mine], y_send, y_recv, device_id=(me, peer), device_id_type=MESH
        ).start()
    pltpu.make_async_copy(cache_turn.at[mine], carried.at[mine], y_recv).start()
    pltpu.make_async_copy(carried, carried, y_recv).wait()

    gain = gn_all[0:1, :].astype(jnp.float32)
    size = slots // stages
    tokens = size * block
    spot = lax.rem(lax.broadcasted_iota(jnp.int32, (steps * tokens, 1), 0), width)

    def encode(i, _):
        stage = stages - 1 - i
        here = pl.ds(stage * size, size)
        pltpu.make_async_copy(rows.at[:, here], rows.at[:, here], f_recv.at[stage]).wait()
        pieces = [rows[m, here].reshape(tokens, lanes) for m in range(ranks)]
        dead = pieces[0][:, 0:1].astype(jnp.float32)
        dead = dead != dead
        pieces = pieces + [carried[m, here].reshape(tokens, lanes) for m in range(ranks)]
        both = jnp.dot(jnp.concatenate(pieces, axis=1), taps[...], preferred_element_type=jnp.float32)
        conv = jnp.concatenate([both[:, :channels], both[:, channels:]], axis=0)
        scale = lax.rsqrt(jnp.sum(conv * conv, axis=1, keepdims=True) / channels + EPS)
        scaled = conv * scale * gain
        active = scaled * (1.0 / (1.0 + jnp.exp(-scaled)))
        before = jnp.where(spot == 0, 0.0, pltpu.roll(active, 1, 0))
        after = jnp.where(spot == width - 1, 0.0, pltpu.roll(active, steps * tokens - 1, 0))
        joined = jnp.concatenate([v.astype(jnp.bfloat16) for v in (before, active, after)], axis=1)
        total = conv + jnp.dot(joined, ws_all[...], preferred_element_type=jnp.float32)
        total = jnp.where(jnp.concatenate([dead] * steps, axis=0), 0.0, total).astype(jnp.bfloat16)
        for m in range(ranks):
            for t in range(steps):
                piece = total[t * tokens : (t + 1) * tokens, m * part : (m + 1) * part]
                result[m, here, :, t] = piece.reshape(size, pair, width, part)
        for turn in range(1, ranks):
            peer = lax.rem(mine + turn, ranks)
            pltpu.make_async_remote_copy(
                result.at[peer, here], out.at[mine, here], o_send, o_recv, device_id=(me, peer), device_id_type=MESH
            ).start()
        pltpu.make_async_copy(result.at[mine, here], out.at[mine, here], o_recv).start()
        return 0

    lax.fori_loop(0, stages, encode, 0)

    for index, (own, whole) in enumerate(weights):
        sent = whole.at[:, pl.ds(0, (ranks - 1) * part)]
        pltpu.make_async_copy(sent, sent, w_send.at[index]).wait()
    pltpu.make_async_copy(cache_out.at[others], cache_out.at[others], c_send).wait()

    @pl.when(mine == 0)
    def _():
        pltpu.make_async_copy(frames_out.at[others], frames_out.at[others], f_send).wait()

    @pl.when(mine != 0)
    def _():
        pltpu.make_async_copy(frames_out, frames_out, f_send).wait()

    sent = cache_turn.at[pl.ds(0, ranks - 1)]
    pltpu.make_async_copy(sent, sent, y_send).wait()
    sent = result.at[pl.ds(0, ranks - 1)]
    pltpu.make_async_copy(sent, sent, o_send).wait()
    slot_store.wait()
    pltpu.make_async_copy(out, out, o_recv).wait()


def order_kernel(slot_of, got, out, held, load_sem, store_sem):
    quarter = held.shape[0] // 4
    loads = [
        pltpu.make_async_copy(
            got.at[pl.ds(i * quarter, quarter)], held.at[pl.ds(i * quarter, quarter)], load_sem.at[i]
        )
        for i in range(4)
    ]
    for load in loads:
        load.start()
    for load in loads:
        load.wait()

    def place(i, _):
        pltpu.make_async_copy(held.at[slot_of[0, i]], out.at[i], store_sem).start()
        return 0

    lax.fori_loop(0, out.shape[0], place, 0)
    pltpu.make_async_copy(held, out, store_sem).wait()


def local(
    owners, ranks,
    frames, cache, group_offset, cache_offset, cache_group, group_rows, cache_live,
    temporal_weight, spatial_weight, norm_gain,
):
    groups = group_offset.shape[0]
    pair = frames.shape[0] // groups
    steps, width, cut = frames.shape[1:]
    channels, part = spatial_weight.shape[1:]
    slots = owners // ranks
    stages = grid_of(owners)[0] * min(2, grid_of(owners)[1] // 4)
    rows_minor = lambda x: jnp.transpose(x, (1, 2, 3, 0)).reshape(steps * width * cut, groups * pair)
    line = lambda x: x.reshape(1, groups)
    block, lanes, tokens = pair * width, steps * cut, pair * steps * width
    smem, hbm = (pl.BlockSpec(memory_space=s) for s in (pltpu.SMEM, pltpu.HBM))
    bf16 = jnp.bfloat16
    dma = pltpu.SemaphoreType.DMA
    got, own_slot = pl.pallas_call(
        functools.partial(exchange_kernel, (owners, ranks, pair, steps, width, cut, channels)),
        out_shape=(
            jax.ShapeDtypeStruct((ranks, slots, pair, steps, width, part), bf16),
            jax.ShapeDtypeStruct((1, groups), jnp.int32),
        ),
        in_specs=[hbm] * 10,
        out_specs=(hbm, hbm),
        scratch_shapes=[
            pltpu.VMEM((5, 1, groups), jnp.int32),
            pltpu.VMEM((1, groups), jnp.int32),
            pltpu.VMEM((1, groups), jnp.int32),
            pltpu.SMEM((1, groups), jnp.int32),
            pltpu.VMEM((owners * block, lanes), jnp.float32),
            pltpu.VMEM((steps * width * cut, groups * pair), bf16),
            pltpu.VMEM((steps * width * cut, groups * pair), bf16),
            pltpu.VMEM((16, part), bf16),
            pltpu.VMEM((1, part), bf16),
            pltpu.VMEM((owners, block, lanes), bf16),
            pltpu.VMEM((owners, block, lanes), bf16),
            pltpu.VMEM((owners, block, lanes), bf16),
            pltpu.VMEM((ranks, slots, block, lanes), bf16),
            pltpu.VMEM((ranks, slots, block, lanes), bf16),
            pltpu.VMEM((ranks, slots, block, lanes), bf16),
            pltpu.VMEM((3 * cut * ranks, channels), bf16),
            pltpu.VMEM((3 * channels, channels), bf16),
            pltpu.VMEM((16, channels), bf16),
            pltpu.VMEM((2 * ranks * lanes, steps * channels), bf16),
            pltpu.VMEM((ranks, slots, pair, steps, width, part), bf16),
            dma((8,)), dma((2,)), dma((3,)), dma((3,)), dma(()), dma(()), dma(()), dma((stages,)),
            dma(()), dma(()), dma(()), dma(()), pltpu.SemaphoreType.REGULAR,
        ],
        compiler_params=pltpu.CompilerParams(
            collective_id=0, has_side_effects=True, vmem_limit_bytes=60 << 20
        ),
        name="exchange",
    )(
        line(group_offset), line(cache_offset), line(cache_group), line(group_rows), line(cache_live),
        rows_minor(cache), rows_minor(frames),
        temporal_weight.reshape(-1, part), spatial_weight.reshape(-1, part), norm_gain.reshape(1, part),
    )
    ordered = pl.pallas_call(
        order_kernel,
        out_shape=jax.ShapeDtypeStruct((groups, tokens, part), bf16),
        in_specs=[smem, hbm],
        out_specs=hbm,
        scratch_shapes=[pltpu.VMEM((groups, tokens, part), bf16), dma((4,)), dma(())],
        compiler_params=pltpu.CompilerParams(vmem_limit_bytes=60 << 20),
        name="order",
    )(own_slot, got.reshape(groups, tokens, part))
    return ordered.reshape(groups * pair, steps, width, part)


def solution(mesh):
    in_specs = (
        P("dp", None, None, "mp"),
        P("dp", None, None, "mp"),
        P(),
        P(),
        P(),
        P("dp", None),
        P("dp"),
        P(None, None, "mp"),
        P(None, None, "mp"),
        P("mp"),
    )
    out_specs = P("dp", None, None, "mp")
    body = functools.partial(local, mesh.shape["dp"], mesh.shape["mp"])
    return jax.shard_map(body, mesh=mesh, in_specs=in_specs, out_specs=out_specs, check_vma=False)
```

```python
import functools

import jax
import jax.numpy as jnp
from jax import lax
from jax.experimental import pallas as pl
from jax.experimental.pallas import tpu as pltpu
from jax.sharding import PartitionSpec as P

MESH = pl.DeviceIdType.MESH
EPS = 1e-6


def grid_of(owners):
    x_size = max(1, owners // 32)
    return x_size, owners // (2 * x_size)


def log2(size):
    return size.bit_length() - 1


def pair_number(source, owner, owners):
    x_size, z_size = grid_of(owners)
    half = z_size // 2
    dc = (owner - source) & 1
    dz = ((owner >> 1) - (source >> 1)) & (z_size - 1)
    dx = ((owner >> log2(2 * z_size)) - (source >> log2(2 * z_size))) & (x_size - 1)
    b = jnp.where(dz >= half, 1, 0)
    h = jnp.where(dz >= half, z_size - 1 - dz, dz)
    c = (dx - h) & (x_size - 1)
    return ((c * half + h) * 2 + dc) * 2 + b


def compute_slot(n, owners, ranks):
    half = grid_of(owners)[1] // 2
    b, dc, h, c = n & 1, (n >> 1) & 1, (n >> 2) & (half - 1), n >> log2(4 * half)
    rank = (c + 2 * dc + ((h + (h >> 1)) & 1)) & (ranks - 1)
    return rank * (owners // ranks) + c * half + (h >> 1) * 2 + b


def exchange_kernel(
    sizes, goes_to, cache_goes_to, continues, counts, lives, xc, xf, wt, ws, gn, out, order_out,
    table, picks, slot_row, slot_of, wide, xc_in, xf_in, gn_own, gn_row,
    cache_out, frames_out, cache_in, cache_turn, carried, rows, wt_all, ws_all, gn_all, taps, result,
    x_sem, t_sem, w_send, w_recv, c_send, c_recv, f_send, f_recv, y_send, y_recv, o_send, o_recv, ready,
):
    owners, ranks, pair, steps, width, cut, channels = sizes
    x_size, z_size = grid_of(owners)
    half = z_size // 2
    slots = owners // ranks
    stages = x_size * half // 2
    part = channels // ranks
    c_in = cut * ranks
    lanes = steps * cut
    block = pair * width
    me, mine = lax.axis_index("dp"), lax.axis_index("mp")
    my_c, my_z, my_x = lax.rem(me, 2), lax.rem(lax.div(me, 2), z_size), lax.div(me, 2 * z_size)
    my_columns = pl.ds(pl.multiple_of(mine * part, part), part)
    bf16, f32 = jnp.bfloat16, jnp.float32

    def split(n):
        if isinstance(n, int):
            return n % 2, n // 2 % 2, n // 4 % half, n // (4 * half)
        return lax.rem(n, 2), lax.rem(lax.div(n, 2), 2), lax.rem(lax.div(n, 4), half), lax.div(n, 4 * half)

    def owner_of(n):
        b, dc, h, c = split(n)
        z = lax.rem(my_z + h + b * (z_size - 1 - 2 * h), z_size)
        x = lax.rem(my_x + c + h, x_size)
        return (x * z_size + z) * 2 + lax.rem(my_c + dc, 2)

    loads = [
        pltpu.make_async_copy(own, here, x_sem.at[i])
        for i, (own, here) in enumerate(
            [(xc, xc_in), (xf, xf_in), (gn, gn_row)]
            + [(v, table.at[i]) for i, v in enumerate((goes_to, cache_goes_to, continues, counts, lives))]
        )
    ]
    for load in loads[3:] + loads[:3]:
        load.start()

    barrier = pltpu.get_barrier_semaphore()

    def greet():
        for i in range(owners - 1):
            turn, low = i // (4 * x_size), i % 4
            n = i // 4 % x_size * (4 * half) + (half - 1 - turn) * 4 + 3 - low
            if turn == half - 1:
                c, low = divmod(i - turn * 4 * x_size, 4) if i < owners - 4 else (x_size - 1, i - owners + 4)
                c = x_size - 1 - c
                n = c * 4 * half + 3 - low
            pl.semaphore_signal(barrier, inc=1, device_id=(owner_of(n), mine), device_id_type=MESH)

    greet()
    for turn in range(1, ranks):
        pl.semaphore_signal(
            barrier, inc=1, device_id=(me, lax.rem(mine + turn, ranks)), device_id_type=MESH
        )

    for load in loads[3:]:
        load.wait()
    group_to, cache_to, group_of, count, live = (table[i] for i in range(5))
    frames_n = pair_number(me, (me + group_to) & (owners - 1), owners)
    cache_n = pair_number(me, (me + cache_to) & (owners - 1), owners)
    sort = lax.broadcasted_iota(jnp.int32, (8, owners), 0)
    stack = jnp.where(sort == 0, frames_n, jnp.where(sort == 1, cache_n, jnp.where(sort == 2, count, live)))
    spread = lax.broadcasted_iota(jnp.int32, (owners, owners * pair), 1) >> log2(pair)
    spread = spread == lax.broadcasted_iota(jnp.int32, (owners, owners * pair), 0)
    one_hot = lambda mask: jnp.where(mask, 1.0, 0.0).astype(bf16)
    keys = jnp.dot(stack.astype(f32).astype(bf16), one_hot(spread), preferred_element_type=f32)
    second = (lax.broadcasted_iota(jnp.int32, (1, owners * pair), 1) & (pair - 1)).astype(f32)
    target = lax.broadcasted_iota(jnp.int32, (owners * pair, owners * pair), 0).astype(f32)

    def pack(x, place, goes):
        for w in range(width):
            columns = jnp.concatenate(
                [x[(t * width + w) * cut : (t * width + w + 1) * cut, :] for t in range(steps)], axis=0
            )
            wide[pl.ds(w, owners * pair, stride=width), :] = lax.dot_general(
                place, columns, (((1,), (1,)), ((), ())), preferred_element_type=f32
            )

        per = min(16, owners)

        def narrow(i, _):
            piece = wide[pl.ds(pl.multiple_of(i * (per * block), per * block), per * block), :]
            goes[pl.ds(i * per, per)] = piece.astype(bf16).reshape(per, block, lanes)
            return 0

        lax.fori_loop(0, owners // per, narrow, 0)

    loads[0].wait()
    pack(xc_in, jnp.where(target == keys[1:2, :] * pair + second, keys[3:4, :], 0.0).astype(bf16), cache_out)

    pl.semaphore_wait(barrier, owners - 1 + ranks - 1)
    for turn in range(1, ranks):
        pl.semaphore_signal(ready, inc=1, device_id=(me, lax.rem(mine + turn, ranks)), device_id_type=MESH)

    def send_cache(i, _):
        n = owners - 1 - i
        pltpu.make_async_remote_copy(
            cache_out.at[n], cache_in.at[n], c_send, c_recv, device_id=(owner_of(n), mine), device_id_type=MESH
        ).start()
        return 0

    lax.fori_loop(0, owners - 1, send_cache, 0)

    loads[1].wait()
    valid = jnp.where(second < keys[2:3, :], 1.0, jnp.nan)
    pack(xf_in, jnp.where(target == keys[0:1, :] * pair + second, valid, 0.0).astype(bf16), frames_out)

    def frames_copy(n):
        b, dc, h, c = split(n)
        rank = lax.rem(c + 2 * dc + lax.rem(h + lax.div(h, 2), 2), ranks)
        place = c * half + lax.div(h, 2) * 2 + b
        return pltpu.make_async_remote_copy(
            frames_out.at[n], rows.at[mine, place], f_send, f_recv.at[lax.div(n, owners // stages)],
            device_id=(owner_of(n), rank), device_id_type=MESH,
        )

    pl.semaphore_wait(ready, ranks - 1)

    def send_frames(i, _):
        frames_copy(owners - 1 - i).start()
        return 0

    lax.fori_loop(0, owners - 1, send_frames, 0)

    @pl.when(mine == 0)
    def _():
        pltpu.make_async_copy(frames_out.at[0], rows.at[0, 0], f_recv.at[0]).start()

    @pl.when(mine != 0)
    def _():
        frames_copy(0).start()

    loads[2].wait()
    gn_own[...] = jnp.broadcast_to(gn_row[...].astype(f32), gn_own.shape).astype(bf16)
    weights = ((wt, wt_all), (ws, ws_all), (gn_own, gn_all))
    for index, (own, whole) in enumerate(weights):
        for turn in range(1, ranks):
            pltpu.make_async_remote_copy(
                own, whole.at[:, my_columns], w_send.at[index], w_recv.at[index],
                device_id=(me, lax.rem(mine + turn, ranks)), device_id_type=MESH,
            ).start()
        pltpu.make_async_copy(own, whole.at[:, my_columns], w_recv.at[index]).start()

    own_n = pair_number((me - group_to) & (owners - 1), me, owners)
    own_slot = compute_slot(own_n, owners, ranks)
    slot_row[...] = own_slot
    slot_store = pltpu.make_async_copy(slot_row, order_out, t_sem.at[1])
    slot_store.start()
    line = lax.broadcasted_iota(jnp.int32, (owners, owners), 0)

    def choose(values, mask):
        values = jnp.broadcast_to(values.astype(f32), (8, owners)).astype(bf16)
        got = lax.dot_general(values, one_hot(mask), (((1,), (1,)), ((), ())), preferred_element_type=f32)
        return got[0:1, :].astype(jnp.int32)

    cache_here = choose(cache_to, line == group_of)
    cache_from = pair_number((me - cache_here) & (owners - 1), me, owners)
    picks[...] = choose(cache_from, line == own_slot)
    pick_load = pltpu.make_async_copy(picks, slot_of, t_sem.at[0])
    pick_load.start()

    for index, (own, whole) in enumerate(weights):
        pltpu.make_async_copy(whole, whole, w_recv.at[index]).wait()
    for m in range(ranks):
        tap = [wt_all[k * c_in + m * cut : k * c_in + (m + 1) * cut, :] for k in range(3)]
        nothing = jnp.zeros_like(tap[0])
        table = ((tap[0], tap[1]), (nothing, tap[0]), (tap[2], nothing), (tap[1], tap[2]))
        for q, (first, second) in enumerate(table):
            start = (q // 2 * ranks + m) * lanes + q % 2 * cut
            taps[start : start + cut, :channels] = first
            taps[start : start + cut, channels:] = second

    others = pl.ds(1, owners - 1)
    pltpu.make_async_copy(cache_in.at[others], cache_in.at[others], c_recv).wait()
    cache_in[0] = cache_out[0]

    pick_load.wait()

    def turn_cache(i, _):
        cache_turn[lax.div(i, slots), lax.rem(i, slots)] = cache_in[jnp.minimum(jnp.maximum(slot_of[0, i], 0), owners - 1)]
        return 0

    lax.fori_loop(0, owners, turn_cache, 0)
    for turn in range(1, ranks):
        peer = lax.rem(mine + turn, ranks)
        pltpu.make_async_remote_copy(
            cache_turn.at[peer], carried.at[mine], y_send, y_recv, device_id=(me, peer), device_id_type=MESH
        ).start()
    pltpu.make_async_copy(cache_turn.at[mine], carried.at[mine], y_recv).start()
    pltpu.make_async_copy(carried, carried, y_recv).wait()

    gain = gn_all[0:1, :].astype(jnp.float32)
    size = slots // stages
    tokens = size * block
    spot = lax.rem(lax.broadcasted_iota(jnp.int32, (steps * tokens, 1), 0), width)

    def encode(i, _):
        stage = stages - 1 - i
        here = pl.ds(stage * size, size)
        pltpu.make_async_copy(rows.at[:, here], rows.at[:, here], f_recv.at[stage]).wait()
        pieces = [rows[m, here].reshape(tokens, lanes) for m in range(ranks)]
        dead = pieces[0][:, 0:1].astype(jnp.float32)
        dead = dead != dead
        pieces = pieces + [carried[m, here].reshape(tokens, lanes) for m in range(ranks)]
        both = jnp.dot(jnp.concatenate(pieces, axis=1), taps[...], preferred_element_type=jnp.float32)
        conv = jnp.concatenate([both[:, :channels], both[:, channels:]], axis=0)
        scale = lax.rsqrt(jnp.sum(conv * conv, axis=1, keepdims=True) / channels + EPS)
        scaled = conv * scale * gain
        active = scaled * (1.0 / (1.0 + jnp.exp(-scaled)))
        before = jnp.where(spot == 0, 0.0, pltpu.roll(active, 1, 0))
        after = jnp.where(spot == width - 1, 0.0, pltpu.roll(active, steps * tokens - 1, 0))
        joined = jnp.concatenate([v.astype(jnp.bfloat16) for v in (before, active, after)], axis=1)
        total = conv + jnp.dot(joined, ws_all[...], preferred_element_type=jnp.float32)
        total = jnp.where(jnp.concatenate([dead] * steps, axis=0), 0.0, total).astype(jnp.bfloat16)
        for m in range(ranks):
            for t in range(steps):
                piece = total[t * tokens : (t + 1) * tokens, m * part : (m + 1) * part]
                result[m, here, :, t] = piece.reshape(size, pair, width, part)
        for turn in range(1, ranks):
            peer = lax.rem(mine + turn, ranks)
            pltpu.make_async_remote_copy(
                result.at[peer, here], out.at[mine, here], o_send, o_recv, device_id=(me, peer), device_id_type=MESH
            ).start()
        pltpu.make_async_copy(result.at[mine, here], out.at[mine, here], o_recv).start()
        return 0

    lax.fori_loop(0, stages, encode, 0)

    for index, (own, whole) in enumerate(weights):
        sent = whole.at[:, pl.ds(0, (ranks - 1) * part)]
        pltpu.make_async_copy(sent, sent, w_send.at[index]).wait()
    pltpu.make_async_copy(cache_out.at[others], cache_out.at[others], c_send).wait()

    @pl.when(mine == 0)
    def _():
        pltpu.make_async_copy(frames_out.at[others], frames_out.at[others], f_send).wait()

    @pl.when(mine != 0)
    def _():
        pltpu.make_async_copy(frames_out, frames_out, f_send).wait()

    sent = cache_turn.at[pl.ds(0, ranks - 1)]
    pltpu.make_async_copy(sent, sent, y_send).wait()
    sent = result.at[pl.ds(0, ranks - 1)]
    pltpu.make_async_copy(sent, sent, o_send).wait()
    slot_store.wait()
    pltpu.make_async_copy(out, out, o_recv).wait()


def order_kernel(slot_of, got, out, held, ordered, load_sem, store_sem):
    load = pltpu.make_async_copy(got, held, load_sem)
    load.start()
    load.wait()
    count = store_sem.shape[0]
    size = held.shape[0] // count

    def place(q, _):
        for i in range(size):
            ordered[q * size + i] = held[slot_of[0, q * size + i]]
        here = pl.ds(q * size, size)
        pltpu.make_async_copy(ordered.at[here], out.at[here], store_sem.at[q]).start()
        return 0

    lax.fori_loop(0, count, place, 0)
    for q in range(count):
        here = pl.ds(q * size, size)
        pltpu.make_async_copy(ordered.at[here], out.at[here], store_sem.at[q]).wait()


def local(
    owners, ranks,
    frames, cache, group_offset, cache_offset, cache_group, group_rows, cache_live,
    temporal_weight, spatial_weight, norm_gain,
):
    groups = group_offset.shape[0]
    pair = frames.shape[0] // groups
    steps, width, cut = frames.shape[1:]
    channels, part = spatial_weight.shape[1:]
    slots = owners // ranks
    stages = grid_of(owners)[0] * grid_of(owners)[1] // 4
    rows_minor = lambda x: jnp.transpose(x, (1, 2, 3, 0)).reshape(steps * width * cut, groups * pair)
    line = lambda x: x.reshape(1, groups)
    block, lanes, tokens = pair * width, steps * cut, pair * steps * width
    smem, hbm = (pl.BlockSpec(memory_space=s) for s in (pltpu.SMEM, pltpu.HBM))
    bf16 = jnp.bfloat16
    dma = pltpu.SemaphoreType.DMA
    got, own_slot = pl.pallas_call(
        functools.partial(exchange_kernel, (owners, ranks, pair, steps, width, cut, channels)),
        out_shape=(
            jax.ShapeDtypeStruct((ranks, slots, pair, steps, width, part), bf16),
            jax.ShapeDtypeStruct((1, groups), jnp.int32),
        ),
        in_specs=[hbm] * 10,
        out_specs=(hbm, hbm),
        scratch_shapes=[
            pltpu.VMEM((5, 1, groups), jnp.int32),
            pltpu.VMEM((1, groups), jnp.int32),
            pltpu.VMEM((1, groups), jnp.int32),
            pltpu.SMEM((1, groups), jnp.int32),
            pltpu.VMEM((owners * block, lanes), jnp.float32),
            pltpu.VMEM((steps * width * cut, groups * pair), bf16),
            pltpu.VMEM((steps * width * cut, groups * pair), bf16),
            pltpu.VMEM((16, part), bf16),
            pltpu.VMEM((1, part), bf16),
            pltpu.VMEM((owners, block, lanes), bf16),
            pltpu.VMEM((owners, block, lanes), bf16),
            pltpu.VMEM((owners, block, lanes), bf16),
            pltpu.VMEM((ranks, slots, block, lanes), bf16),
            pltpu.VMEM((ranks, slots, block, lanes), bf16),
            pltpu.VMEM((ranks, slots, block, lanes), bf16),
            pltpu.VMEM((3 * cut * ranks, channels), bf16),
            pltpu.VMEM((3 * channels, channels), bf16),
            pltpu.VMEM((16, channels), bf16),
            pltpu.VMEM((2 * ranks * lanes, steps * channels), bf16),
            pltpu.VMEM((ranks, slots, pair, steps, width, part), bf16),
            dma((8,)), dma((2,)), dma((3,)), dma((3,)), dma(()), dma(()), dma(()), dma((stages,)),
            dma(()), dma(()), dma(()), dma(()), pltpu.SemaphoreType.REGULAR,
        ],
        compiler_params=pltpu.CompilerParams(
            collective_id=0, has_side_effects=True, vmem_limit_bytes=60 << 20
        ),
        name="exchange",
    )(
        line(group_offset), line(cache_offset), line(cache_group), line(group_rows), line(cache_live),
        rows_minor(cache), rows_minor(frames),
        temporal_weight.reshape(-1, part), spatial_weight.reshape(-1, part), norm_gain.reshape(1, part),
    )
    ordered = pl.pallas_call(
        order_kernel,
        out_shape=jax.ShapeDtypeStruct((groups, tokens, part), bf16),
        in_specs=[smem, hbm],
        out_specs=hbm,
        scratch_shapes=[pltpu.VMEM((groups, tokens, part), bf16)] * 2 + [dma(()), dma((4,))],
        compiler_params=pltpu.CompilerParams(vmem_limit_bytes=60 << 20),
        name="order",
    )(own_slot, got.reshape(groups, tokens, part))
    return ordered.reshape(groups * pair, steps, width, part)


def solution(mesh):
    in_specs = (
        P("dp", None, None, "mp"),
        P("dp", None, None, "mp"),
        P(),
        P(),
        P(),
        P("dp", None),
        P("dp"),
        P(None, None, "mp"),
        P(None, None, "mp"),
        P("mp"),
    )
    out_specs = P("dp", None, None, "mp")
    body = functools.partial(local, mesh.shape["dp"], mesh.shape["mp"])
    return jax.shard_map(body, mesh=mesh, in_specs=in_specs, out_specs=out_specs, check_vma=False)
```
